32 devices in a mesh: context: 16 (over z, x, core), heads: 2 (over y).
Axes of the slice: x: 2, y: 2, z: 4, core: 2. Of those that a mesh axis runs over, the one named last changes fastest.
Arguments:
- residual: bfloat16 [2048, 2880], P('context'), may hold values from -6 to 6
- query_rows: bfloat16 [2048, 3584], P('context', 'heads'), may hold values from -6 to 6
- key_rows: bfloat16 [2048, 3584], P('context', 'heads'), may hold values from -6 to 6
- value_rows: bfloat16 [2048, 3584], P('context', 'heads'), may hold values from -6 to 6
- norm_gain: float32 [3584], P('heads'), may hold values from 0.1 to 1.9
- out_weight: bfloat16 [3584, 2880], P('heads'), may hold values from -0.09375 to 0.09375
- moe_gain: float32 [2880], replicated, may hold values from 0.1 to 1.9
- expert_ids: int32 [2048, 4], P('context'), may hold values from 0 to 7, all different within a row; in each aligned block of 128 rows (0 to 127, 128 to 255, ...) at most 96 rows name the same one
- gate_values: float32 [2048, 4], P('context'), may hold values from 0.2 to 1
- gate_weight: bfloat16 [16, 2880, 1440], P('context', None, 'heads'), may hold values from -0.109375 to 0.109375
- up_weight: bfloat16 [16, 2880, 1440], P('context', None, 'heads'), may hold values from -0.109375 to 0.109375
- down_weight: bfloat16 [16, 1440, 2880], P('context', 'heads'), may hold values from -0.109375 to 0.109375
Outputs:
- layer_out: bfloat16 [2048, 2880], P(('context', 'heads'))
The draws below stay inside these ranges and needn't reach their ends.
Inputs may be any that keep to these rules, and one draw needn't show every extreme that they name: `expert_ids`: each token names 4 different experts. Among the 128 tokens of one block at most 96 name the same expert, and in every draw some expert is named by exactly 96 tokens of some block.
All inputs are finite; a program needn't handle non-finite values.
Results may differ from the reference program's by a relative error of at most 0.017.
Values may be sent and summed in bfloat16 or wider, within the bound.
A program may use at most 128 MiB of HBM per device.

```python
import math
import jax
import jax.numpy as jnp
import numpy as np
from jax import lax

D = 2880
FF = 2880
HEADS = 56
HD = 64
TOP = 4
CSPLIT = 2
TOK_DEV = 128
TOKENS = 2048
EXPERTS = 8
HSPLIT = 4
FF_DEV = 720
CAP = 96
N_CONTEXT = 16


def level_of(rng, dims, pieces, smallest, largest):
    gain, own = 1.0, jax.random.fold_in(rng, 6)
    for axis_at, parts in pieces:
        steps = jnp.exp(jax.random.uniform(jax.random.fold_in(own, axis_at), (parts,), jnp.float32, smallest / len(pieces), largest / len(pieces)))
        gain = gain * jnp.repeat(steps, dims[axis_at] // parts).reshape([-1 if axis == axis_at else 1 for axis in range(len(dims))])
    return gain


def assign_block(stream_key, own, number, rows, number_of, top, limit, slope):
    order = jax.random.permutation(stream_key, number_of)
    heavy_load, ordinary = shares(number_of, rows * top, limit, slope, True), shares(number_of, rows * top, limit, slope, False)
    places = jnp.arange(number_of)

    def named(lengths, turn):
        used = int((lengths > 0).sum())
        fixed = max(1, used // 4)
        shifted = fixed + (places - fixed + turn * (used - fixed)) % max(1, number_of - fixed)
        return jnp.zeros((number_of,), jnp.int32).at[order[jnp.where(places < fixed, places, shifted)]].set(jnp.asarray(lengths, jnp.int32))

    lengths = jnp.where(number % 4 == 0, named(heavy_load, number // 4), named(ordinary, number - number // 4 - 1))
    mixed = jax.random.permutation(jax.random.fold_in(own, 3), number_of)
    source_of, receiver = mixed[0:number_of // 2 * 2:2], mixed[1:number_of // 2 * 2:2]
    room = jnp.minimum(lengths[source_of] - 1, limit - lengths[receiver]) // 2
    room = jnp.where((source_of == order[0]) | (receiver == order[0]) | (lengths[receiver] == 0), 0, jnp.maximum(room, 0))
    shifted = jax.random.randint(jax.random.fold_in(own, 4), (number_of // 2,), 0, 1 << 20) % (room + 1)
    lengths = lengths.at[source_of].add(-shifted).at[receiver].add(shifted)
    members = jnp.searchsorted(jnp.cumsum(lengths), jnp.arange(rows * top), side="right").astype(jnp.int32)
    grid = members.reshape(top, rows).T
    grid = grid[jax.random.permutation(jax.random.fold_in(own, 1), rows)]
    turn = jax.random.randint(jax.random.fold_in(own, 2), (rows, 1), 0, top)
    return jnp.take_along_axis(grid, (jnp.arange(top)[None, :] + turn) % top, axis=1)


def shares(amount, total, bound, slope, full):
    loads = [(1 << 20) // math.isqrt(standing ** slope) + 1 for standing in range(1, amount + 1)]
    largest = bound if full else min(bound, max(-(-total // amount), total * loads[0] // sum(loads)))
    least = 1 if total - largest >= amount - 1 else 0
    given, spare = [largest] + [least] * (amount - 1), total - largest - least * (amount - 1)
    while spare > 0:
        movable = [i for i in range(1, amount) if given[i] < largest] or [i for i in range(1, amount) if given[i] < bound]
        whole, left = sum([loads[i] for i in movable]), spare
        for i in movable:
            more = min(bound - given[i], max(1, left * loads[i] // whole), spare)
            given[i] = given[i] + more
            spare = spare - more
    return np.array(given)


def noise(stream_key, extent, width, most, shards=(), kind=jnp.bfloat16):
    array = width * jax.random.normal(stream_key, extent, jnp.float32)
    if shards:
        array = array * level_of(stream_key, extent, shards, -0.22, 0.18)
    return jnp.clip(array, -most, most).astype(kind)


def setup_inputs(seed: int = 0) -> dict:
    splits = jax.random.split(jax.random.key(seed), 13)
    residual = noise(splits[0], (TOKENS, D), 1.0, 6.0, ((0, 16),))
    query_rows = noise(splits[1], (TOKENS, HEADS * HD), 1.0, 6.0, ((0, 16), (1, 2)))
    key_rows = noise(splits[2], (TOKENS, HEADS * HD), 1.0, 6.0, ((0, 16), (1, 2)))
    value_rows = noise(splits[3], (TOKENS, HEADS * HD), 1.0, 6.0, ((0, 16), (1, 2)))
    norm_gain = jnp.clip(1.0 + 0.18 * jax.random.normal(splits[4], (HEADS * HD,), jnp.float32), 0.1, 1.9)
    out_weight = noise(splits[5], (HEADS * HD, D), (HEADS * HD) ** -0.5, 0.09375, ((0, 2),))
    moe_gain = jnp.clip(1.0 + 0.18 * jax.random.normal(splits[6], (D,), jnp.float32), 0.1, 1.9)
    expert_ids_keys = jax.random.split(jax.random.fold_in(splits[7], 1), TOKENS // TOK_DEV)
    expert_ids_turns = jax.random.permutation(jax.random.fold_in(splits[7], 3), TOKENS // TOK_DEV)
    expert_ids = jax.vmap(lambda own, number: assign_block(jax.random.fold_in(splits[7], 2), own, number, TOK_DEV, EXPERTS, TOP, CAP, 1))(expert_ids_keys, expert_ids_turns).reshape((TOKENS, TOP))
    gate_values = jnp.clip(0.2 + 0.8 * jax.random.uniform(splits[8], (TOKENS, TOP), jnp.float32) ** level_of(splits[8], (TOKENS, TOP), ((0, 16),), -0.2, 0.2), 0.2, 1.0)
    gate_weight = noise(splits[9], (EXPERTS * CSPLIT, D, FF // CSPLIT), D ** -0.5, 0.109375, ((0, 16), (2, 2)))
    up_weight = noise(splits[10], (EXPERTS * CSPLIT, D, FF // CSPLIT), D ** -0.5, 0.109375, ((0, 16), (2, 2)))
    down_weight = noise(splits[11], (EXPERTS * CSPLIT, FF // CSPLIT, D), FF ** -0.5, 0.109375, ((0, 16), (1, 2)))
    return dict(residual=residual, query_rows=query_rows, key_rows=key_rows, value_rows=value_rows, norm_gain=norm_gain, out_weight=out_weight, moe_gain=moe_gain, expert_ids=expert_ids, gate_values=gate_values, gate_weight=gate_weight, up_weight=up_weight, down_weight=down_weight)


def round_trip(values_in):
    lowered = values_in.astype(jnp.bfloat16)
    lowered = lax.optimization_barrier(lowered)
    return lowered.astype(jnp.float32)

def block_attention(query_rows, key_rows, value_rows):
    shaped = (N_CONTEXT, TOK_DEV, HEADS, HD)
    query_blocks = query_rows.reshape(shaped)
    key_blocks = key_rows.reshape(shaped)
    value_blocks = value_rows.reshape(shaped)
    causal = jnp.arange(TOK_DEV)[:, None] >= jnp.arange(TOK_DEV)[None, :]

    def advance(carried, block_set):
        query_wide = block_set[0].astype(jnp.float32)
        key_wide = block_set[1].astype(jnp.float32)
        value_wide = block_set[2].astype(jnp.float32)
        scores = jnp.einsum('thd,shd->hts', query_wide, key_wide)
        weights = round_trip(jnp.where(causal[None], scores, 0.0))
        inner_part = jnp.einsum('hts,shd->thd', weights, value_wide)
        outer_part = jnp.einsum('thd,hde->the', query_wide, round_trip(carried))
        own_state = jnp.einsum('shd,she->hde', key_wide, value_wide)
        return (carried + own_state, inner_part + outer_part)
    initial = jnp.zeros((HEADS, HD, HD), jnp.float32)
    last_state, mixed = lax.scan(advance, initial, (query_blocks, key_blocks, value_blocks))
    return mixed.reshape(TOKENS, HEADS, HD)

def slot_ranks(expert_ids):
    flattened = expert_ids.reshape(N_CONTEXT, TOK_DEV * TOP)
    onehot = (flattened[:, :, None] == jnp.arange(EXPERTS, dtype=jnp.int32)[None, None, :]).astype(jnp.int32)
    before = jnp.cumsum(onehot, axis=1) - onehot
    return lax.optimization_barrier(jnp.sum(before * onehot, axis=2)).reshape(TOKENS, TOP).astype(jnp.int32)

def expert_rows(token_rows, gate_part, up_part, down_part):
    gate_act = jnp.dot(token_rows, gate_part, preferred_element_type=jnp.float32)
    up_act = jnp.dot(token_rows, up_part, preferred_element_type=jnp.float32)
    hidden = (jax.nn.silu(gate_act) * up_act).astype(jnp.bfloat16)
    grouped = hidden.reshape(token_rows.shape[0], HSPLIT, FF_DEV).astype(jnp.float32)
    down_grouped = down_part.reshape(HSPLIT, FF_DEV, D).astype(jnp.float32)
    partial_value = jnp.einsum('rgf,gfd->rgd', grouped, down_grouped)
    return lax.optimization_barrier(jnp.sum(round_trip(partial_value), axis=1))

def run_expert(packed_item):
    return expert_rows(packed_item[0], packed_item[1], packed_item[2], packed_item[3])

def reference(residual, query_rows, key_rows, value_rows, norm_gain, out_weight, moe_gain, expert_ids, gate_values, gate_weight, up_weight, down_weight):
    mixed = block_attention(query_rows, key_rows, value_rows)
    center = lax.optimization_barrier(jnp.mean(mixed, axis=-1, keepdims=True))
    spread = lax.optimization_barrier(jnp.mean(jnp.square(mixed - center), axis=-1, keepdims=True))
    heads_normed = ((mixed - center) * lax.rsqrt(spread + 1e-05) * norm_gain.reshape(HEADS, HD)).astype(jnp.bfloat16)
    attended = residual.astype(jnp.float32) + jnp.dot(heads_normed.reshape(TOKENS, HEADS * HD), out_weight, preferred_element_type=jnp.float32)
    scaling = lax.rsqrt(lax.optimization_barrier(jnp.mean(jnp.square(attended), axis=-1, keepdims=True)) + 1e-06)
    moe_in = (attended * scaling * moe_gain).astype(jnp.bfloat16)
    ranks = slot_ranks(expert_ids)
    block_index = (jnp.arange(TOKENS, dtype=jnp.int32) // TOK_DEV).astype(jnp.int32)[:, None]
    slot_rows = (block_index * CAP + ranks).astype(jnp.int32)
    buffers = jnp.zeros((EXPERTS, N_CONTEXT * CAP, D), jnp.bfloat16)
    buffers = buffers.at[expert_ids, slot_rows].set(jnp.broadcast_to(moe_in[:, None, :], (TOKENS, TOP, D)))
    half_width = FF // CSPLIT
    gate_full = gate_weight.reshape(EXPERTS, CSPLIT, D, half_width).transpose(0, 2, 1, 3).reshape(EXPERTS, D, FF)
    up_full = up_weight.reshape(EXPERTS, CSPLIT, D, half_width).transpose(0, 2, 1, 3).reshape(EXPERTS, D, FF)
    down_full = down_weight.reshape(EXPERTS, FF, D)
    results = lax.map(run_expert, (buffers, gate_full, up_full, down_full))
    picked = results[expert_ids, slot_rows]
    mixture = lax.optimization_barrier(jnp.sum(gate_values[:, :, None] * picked, axis=1))
    return (attended + mixture).astype(jnp.bfloat16)
```

```python
import jax
import jax.numpy as jnp
from jax import lax
from jax.sharding import PartitionSpec as P

HD = 64
CSPLIT = 2


def partner_2(value, axis, apart):
    mask = 2**apart
    pairs = [(source, source ^ mask) for source in range(lax.axis_size(axis))]
    return lax.ppermute(value, axis, pairs)


def grid_of():
    across = lax.axis_size("heads")
    along = lax.axis_size("context") // (CSPLIT * across)
    index = lax.axis_index("context")
    return along, across, index // (CSPLIT * across), index // CSPLIT % across, index % CSPLIT


def from_offset(value, dz, dx, dc, wrap=True):
    along, across = grid_of()[:2]
    pairs = []
    for z in range(along):
        for x in range(across):
            for core in range(CSPLIT):
                if not wrap and not 0 <= z + dz < along:
                    continue
                source = (((z + dz) % along) * across + (x + dx) % across) * CSPLIT
                source += (core + dc) % CSPLIT
                pairs.append((source, (z * across + x) * CSPLIT + core))
    return lax.ppermute(value, "context", pairs)


def from_heads(value, d):
    count = lax.axis_size("heads")
    return lax.ppermute(value, "heads", [((h + d) % count, h) for h in range(count)])


def entering(own):
    along, across, z, x, core = grid_of()
    f32, low = jnp.float32, jnp.bfloat16
    heads = own.shape[0] // 2
    packed = jnp.concatenate([own[:heads], own[heads:]], axis=-1).astype(low)
    other = from_offset(packed, 0, 0, 1)
    before = jnp.where(core == 1, other, jnp.zeros_like(other)).astype(f32)
    pair = packed.astype(f32) + other.astype(f32)
    rows = packed.shape[1] // CSPLIT
    total = lax.dynamic_slice_in_dim(pair, core * rows, rows, 1)
    half = total.astype(low)
    earlier = jnp.zeros_like(total)
    for d in range(1, across):
        part = from_offset(half, 0, d, 0).astype(f32)
        total = total + part
        earlier = earlier + jnp.where(x + d >= across, part, 0.0)
    plane = total.astype(low)
    for d in range(1, along):
        earlier = earlier + from_offset(plane, -d, 0, 0, wrap=False).astype(f32)
    mine = earlier.astype(low)
    theirs = from_offset(mine, 0, 0, 1)
    lower = jnp.where(core == 0, mine, theirs)
    upper = jnp.where(core == 0, theirs, mine)
    before = (before + jnp.concatenate([lower, upper], axis=1).astype(f32)).astype(low)
    return jnp.concatenate([before[:, :, :HD], before[:, :, HD:]], axis=0)


def heads_scattered(partial, share):
    count, me = lax.axis_size("heads"), lax.axis_index("heads")
    total = lax.dynamic_slice_in_dim(partial, me * share, share, 0)
    low = partial.astype(jnp.bfloat16)
    for d in range(1, count):
        start = (me + count - d) % count * share
        sent = lax.dynamic_slice_in_dim(low, start, share, 0)
        total = total + from_heads(sent, d).astype(jnp.float32)
    return total


def steps_of(kind):
    along, across = grid_of()[:2]
    count = {"z": along, "x": across, "y": lax.axis_size("heads"), "c": CSPLIT}[kind]

    def step(value, d):
        if kind == "y":
            return from_heads(value, d)
        return from_offset(value, *[d if kind == name else 0 for name in "zxc"])

    return count, step


def gathered(rows, order):
    parts = [rows]
    for kind in order:
        count, step = steps_of(kind)
        block = parts[0] if len(parts) == 1 else jnp.concatenate(parts, axis=0)
        parts = [block] + [step(block, d) for d in range(1, count)]
    return parts


def added(parts):
    total = parts[0].astype(jnp.float32)
    for part in parts[1:]:
        total = total + part.astype(jnp.float32)
    return total


def scattered(parts, order):
    for kind in reversed(order):
        count, step = steps_of(kind)
        if not isinstance(parts, list):
            rows = parts.shape[0] // count
            parts = [parts[d * rows : (d + 1) * rows] for d in range(count)]
        total = added([parts[0]] + [step(parts[d], count - d) for d in range(1, count)])
        parts = total.astype(jnp.bfloat16) if kind != order[0] else total
    return parts


def gates_of(everyone, order, piece):
    where = {"z": 0, "x": 1, "c": 2, "y": 3}
    kept = everyone[:, :, :, :, piece]
    last_first = [where[kind] for kind in reversed(order)]
    return jnp.transpose(kept, last_first + [4, 5])


def dense_experts(moe_in, expert_ids, gate_values, gate_weight, up_weight, down_weight):
    along, across, z, x, core = grid_of()
    f32, low = jnp.float32, jnp.bfloat16
    context, heads = lax.axis_size("context"), lax.axis_size("heads")
    experts = context // CSPLIT
    named = jnp.arange(experts, dtype=jnp.int32)[None, None, :] == expert_ids[:, :, None]
    gates = jnp.sum(jnp.where(named, gate_values[:, :, None], 0.0), axis=1)
    gates = lax.all_gather(gates, "context", tiled=True)
    expert = lax.axis_index("context") // CSPLIT
    mine = jnp.arange(experts, dtype=jnp.int32)[None, :] == expert
    everyone = jnp.sum(jnp.where(mine, gates, 0.0), axis=1, keepdims=True)
    orders = ("zxyc", "yzxc")
    rows = moe_in.shape[0] // len(orders)
    everyone = everyone.reshape(along, across, CSPLIT, heads, len(orders), rows, 1)
    for axis, place in ((0, z), (1, x), (2, core), (3, lax.axis_index("heads"))):
        everyone = jnp.roll(everyone, -place, axis=axis)

    def expert_rows(token_rows, weight):
        gate_act = jnp.dot(token_rows, gate_weight, preferred_element_type=f32)
        up_act = jnp.dot(token_rows, up_weight, preferred_element_type=f32)
        hidden = (jax.nn.silu(gate_act) * up_act).astype(low)
        out = jnp.dot(hidden, down_weight, preferred_element_type=f32)
        return (out * weight).astype(low)

    sums = []
    for piece, order in enumerate(orders):
        weights = gates_of(everyone, order, piece)
        third = steps_of(order[2])[0]
        weights = weights.reshape(CSPLIT, third, -1, 1)
        early = gathered(moe_in[piece * rows : (piece + 1) * rows], order[:3])
        own, far = [], []
        for d, block in enumerate(early):
            own.append(expert_rows(block, weights[0, d]))
            far.append(expert_rows(from_offset(block, 0, 0, 1), weights[1, d]))
        joined = [
            added([kept, from_offset(sent, 0, 0, 1)]).astype(low)
            for kept, sent in zip(own, far)
        ]
        sums.append(scattered(joined, order[:3]))
    return jnp.concatenate(sums, axis=0)


def rms_scaled(hidden_in, moe_gain):
    scaling = lax.rsqrt(jnp.mean(jnp.square(hidden_in), axis=-1, keepdims=True) + 1e-06)
    return (hidden_in * scaling * moe_gain).astype(jnp.bfloat16)


def on_device(
    residual,
    query_rows,
    key_rows,
    value_rows,
    norm_gain,
    out_weight,
    moe_gain,
    expert_ids,
    gate_values,
    gate_weight,
    up_weight,
    down_weight,
):
    token_count = query_rows.shape[0]
    head_count = query_rows.shape[1] // HD
    query_heads = query_rows.reshape(token_count, head_count, HD)
    key_heads = key_rows.reshape(token_count, head_count, HD)
    value_heads = value_rows.reshape(token_count, head_count, HD)
    own_state = jnp.einsum(
        "shd,she->hde", key_heads, value_heads, preferred_element_type=jnp.float32
    )
    carried = entering(own_state)
    scores = jnp.einsum("thd,shd->hts", query_heads, key_heads, preferred_element_type=jnp.float32)
    causal = jnp.arange(token_count)[:, None] >= jnp.arange(token_count)[None, :]
    weights = jnp.where(causal[None], scores, 0.0).astype(jnp.bfloat16)
    inner_part = jnp.einsum(
        "hts,shd->thd", weights, value_heads, preferred_element_type=jnp.float32
    )
    outer_part = jnp.einsum(
        "thd,hde->the",
        query_heads,
        carried,
        preferred_element_type=jnp.float32,
    )
    mixed = inner_part + outer_part
    center = jnp.mean(mixed, axis=-1, keepdims=True)
    spread = jnp.mean(jnp.square(mixed - center), axis=-1, keepdims=True)
    heads_normed = (
        (mixed - center) * lax.rsqrt(spread + 1e-05) * norm_gain.reshape(head_count, HD)
    ).astype(jnp.bfloat16)
    heads_normed = heads_normed.reshape(token_count, head_count * HD)
    partial_value = jnp.dot(heads_normed, out_weight, preferred_element_type=jnp.float32)
    share = token_count // lax.axis_size("heads")
    offset = lax.axis_index("heads") * share
    if lax.axis_size("context") // CSPLIT <= 2 * expert_ids.shape[1]:
        attended = lax.dynamic_slice_in_dim(residual, offset, share, 0).astype(jnp.float32)
        attended = attended + heads_scattered(partial_value, share)
        moe_part = dense_experts(
            rms_scaled(attended, moe_gain),
            expert_ids,
            gate_values,
            gate_weight[0],
            up_weight[0],
            down_weight[0],
        )
        return (attended + moe_part).astype(jnp.bfloat16)
    attended_all = residual.astype(jnp.float32) + lax.psum(
        partial_value.astype(jnp.bfloat16), "heads"
    ).astype(jnp.float32)
    moe_in = rms_scaled(attended_all, moe_gain)
    attended = lax.dynamic_slice_in_dim(attended_all, offset, share, 0)
    pair_count = CSPLIT
    expert_count = lax.axis_size("context") // CSPLIT
    top_count = expert_ids.shape[1]
    feature_count = moe_in.shape[1]
    capacity = min(token_count, 3 * token_count * top_count // (2 * expert_count))
    flattened = expert_ids.reshape(-1)
    onehot = (flattened[:, None] == jnp.arange(expert_count, dtype=jnp.int32)[None, :]).astype(
        jnp.int32
    )
    ranks = jnp.sum((jnp.cumsum(onehot, axis=0) - onehot) * onehot, axis=1).reshape(
        token_count, top_count
    )
    positions = expert_ids * capacity + ranks
    placer = jnp.any(
        jnp.arange(expert_count * capacity, dtype=jnp.int32)[:, None, None] == positions[None],
        axis=2,
    ).astype(jnp.bfloat16)
    packed = jnp.dot(placer, moe_in, preferred_element_type=jnp.float32).astype(jnp.bfloat16)
    packed = packed.reshape(expert_count, capacity, feature_count)
    half_cap = capacity // pair_count
    outgoing = packed.reshape(expert_count * pair_count, half_cap, feature_count)
    arrived = lax.all_to_all(outgoing, "context", split_axis=0, concat_axis=0, tiled=True)
    partner = partner_2(arrived, "context", 0)
    lower = lax.axis_index("context") % 2 == 0
    first_half = jnp.where(lower, arrived, partner)
    second_half = jnp.where(lower, partner, arrived)
    arrived = jnp.stack([first_half, second_half], axis=2)
    token_rows = arrived.reshape(-1, arrived.shape[-1])
    gate_act = jnp.dot(token_rows, gate_weight[0], preferred_element_type=jnp.float32)
    up_act = jnp.dot(token_rows, up_weight[0], preferred_element_type=jnp.float32)
    hidden = (jax.nn.silu(gate_act) * up_act).astype(jnp.bfloat16)
    partial_rows = jnp.dot(hidden, down_weight[0], preferred_element_type=jnp.float32).astype(
        jnp.bfloat16
    )
    returned = lax.all_to_all(
        partial_rows.reshape(arrived.shape), "context", split_axis=0, concat_axis=0, tiled=True
    )
    slot_offset = ranks % half_cap * pair_count + ranks // half_cap
    flat_return = returned.reshape(-1, feature_count)
    member = jnp.arange(pair_count, dtype=jnp.int32)
    row_index = (
        expert_ids[:, :, None] * pair_count + member[None, None, :]
    ) * capacity + slot_offset[:, :, None]
    picked = jnp.take(flat_return, row_index.reshape(-1), axis=0).reshape(
        token_count, top_count * pair_count, feature_count
    )
    mix_weights = jnp.repeat(gate_values, pair_count, axis=1)
    mixture = jnp.sum(mix_weights[:, :, None] * picked.astype(jnp.float32), axis=1)
    moe_part = lax.psum_scatter(
        mixture.astype(jnp.bfloat16), "heads", scatter_dimension=0, tiled=True
    ).astype(jnp.float32)
    return (attended + moe_part).astype(jnp.bfloat16)


def solution(mesh):
    in_specs = (
        P("context", None),
        P("context", "heads"),
        P("context", "heads"),
        P("context", "heads"),
        P("heads"),
        P("heads", None),
        P(),
        P("context", None),
        P("context", None),
        P("context", None, "heads"),
        P("context", None, "heads"),
        P("context", "heads", None),
    )
    out_specs = P(("context", "heads"), None)
    return jax.shard_map(
        on_device, mesh=mesh, in_specs=in_specs, out_specs=out_specs, check_vma=False
    )
```

```python
import jax
import jax.numpy as jnp
from jax import lax
from jax.experimental import pallas as pl
from jax.experimental.pallas import tpu as pltpu
from jax.sharding import PartitionSpec as P

HD = 64
CSPLIT = 2
LANES = 128


def partner_2(value, axis, apart):
    mask = 2**apart
    pairs = [(source, source ^ mask) for source in range(lax.axis_size(axis))]
    return lax.ppermute(value, axis, pairs)


def grid_of():
    across = lax.axis_size("heads")
    along = lax.axis_size("context") // (CSPLIT * across)
    index = lax.axis_index("context")
    return along, across, index // (CSPLIT * across), index // CSPLIT % across, index % CSPLIT


def from_offset(value, dz, dx, dc, wrap=True):
    along, across = grid_of()[:2]
    pairs = []
    for z in range(along):
        for x in range(across):
            for core in range(CSPLIT):
                if not wrap and not 0 <= z + dz < along:
                    continue
                source = (((z + dz) % along) * across + (x + dx) % across) * CSPLIT
                source += (core + dc) % CSPLIT
                pairs.append((source, (z * across + x) * CSPLIT + core))
    return lax.ppermute(value, "context", pairs)


def from_heads(value, d):
    count = lax.axis_size("heads")
    return lax.ppermute(value, "heads", [((h + d) % count, h) for h in range(count)])


def entering(own):
    along, across, z, x, core = grid_of()
    f32, low = jnp.float32, jnp.bfloat16
    heads = own.shape[0] // 2
    packed = jnp.concatenate([own[:heads], own[heads:]], axis=-1).astype(low)
    other = from_offset(packed, 0, 0, 1)
    before = jnp.where(core == 1, other, jnp.zeros_like(other)).astype(f32)
    pair = packed.astype(f32) + other.astype(f32)
    rows = packed.shape[1] // CSPLIT
    total = lax.dynamic_slice_in_dim(pair, core * rows, rows, 1)
    half = total.astype(low)
    earlier = jnp.zeros_like(total)
    for d in range(1, across):
        part = from_offset(half, 0, d, 0).astype(f32)
        total = total + part
        earlier = earlier + jnp.where(x + d >= across, part, 0.0)
    plane = total.astype(low)
    for d in range(1, along):
        earlier = earlier + from_offset(plane, -d, 0, 0, wrap=False).astype(f32)
    mine = earlier.astype(low)
    theirs = from_offset(mine, 0, 0, 1)
    lower = jnp.where(core == 0, mine, theirs)
    upper = jnp.where(core == 0, theirs, mine)
    before = (before + jnp.concatenate([lower, upper], axis=1).astype(f32)).astype(low)
    return jnp.concatenate([before[:, :, :HD], before[:, :, HD:]], axis=0)


def heads_scattered(partial, share):
    count, me = lax.axis_size("heads"), lax.axis_index("heads")
    total = lax.dynamic_slice_in_dim(partial, me * share, share, 0)
    low = partial.astype(jnp.bfloat16)
    for d in range(1, count):
        start = (me + count - d) % count * share
        sent = lax.dynamic_slice_in_dim(low, start, share, 0)
        total = total + from_heads(sent, d).astype(jnp.float32)
    return total


def steps_of(kind):
    along, across = grid_of()[:2]
    count = {"z": along, "x": across, "y": lax.axis_size("heads"), "c": CSPLIT}[kind]

    def step(value, d):
        if kind == "y":
            return from_heads(value, d)
        return from_offset(value, *[d if kind == name else 0 for name in "zxc"])

    return count, step


def gathered(rows, order):
    parts = [rows]
    for kind in order:
        count, step = steps_of(kind)
        block = parts[0] if len(parts) == 1 else jnp.concatenate(parts, axis=0)
        parts = [block] + [step(block, d) for d in range(1, count)]
    return parts


def added(parts):
    total = parts[0].astype(jnp.float32)
    for part in parts[1:]:
        total = total + part.astype(jnp.float32)
    return total


def scattered(parts, order):
    for kind in reversed(order):
        count, step = steps_of(kind)
        if not isinstance(parts, list):
            rows = parts.shape[0] // count
            parts = [parts[d * rows : (d + 1) * rows] for d in range(count)]
        total = added([parts[0]] + [step(parts[d], count - d) for d in range(1, count)])
        parts = total.astype(jnp.bfloat16) if kind != order[0] else total
    return parts


def expert_kernel(near, far, pick, gate, up, down, near_out, far_out, total):
    step, last = pl.program_id(0), pl.num_programs(0) - 1
    width = gate.shape[1]
    edge = width // LANES * LANES
    f32 = jnp.float32
    across = (((1,), (1,)), ((), ()))
    for turn, (rows, out) in enumerate(((near, near_out), (far, far_out))):
        tokens = rows[:, :width]
        gate_act = lax.dot_general(tokens, gate[...], across, preferred_element_type=f32)
        up_act = lax.dot_general(tokens, up[...], across, preferred_element_type=f32)
        hidden = (gate_act / (1.0 + jnp.exp(-gate_act)) * up_act).astype(jnp.bfloat16)
        part = jnp.dot(hidden, down[...], preferred_element_type=f32)

        @pl.when(step == 0)
        def _():
            total[turn] = part

        @pl.when(step > 0)
        def _():
            total[turn] += part

        @pl.when(step == last)
        def _():
            weight = rows[:, edge:].astype(f32) * pick[...]
            weight = jnp.sum(weight, axis=1, keepdims=True)
            out[...] = (total[turn] * weight).astype(out.dtype)


def expert_rows(near, far, pick, gate, up, down):
    units, width = down.shape
    tile = max(t for t in range(16, 257, 16) if units % t == 0)
    fixed = lambda shape: pl.BlockSpec(shape, lambda i: (0, 0), pipeline_mode=pl.Buffered(1))
    tiles = pl.BlockSpec((tile, width), lambda i: (i, 0))
    count = near.shape[0]
    result = jax.ShapeDtypeStruct((count, width), jnp.bfloat16)
    return pl.pallas_call(
        expert_kernel,
        grid=(units // tile,),
        in_specs=[fixed(near.shape), fixed(far.shape), fixed(pick.shape), tiles, tiles, tiles],
        out_specs=[fixed(result.shape)] * 2,
        out_shape=[result] * 2,
        scratch_shapes=[pltpu.VMEM((2, count, width), jnp.float32)],
        compiler_params=pltpu.CompilerParams(vmem_limit_bytes=48 * 2**20),
        cost_estimate=pl.CostEstimate(
            flops=12 * count * units * width,
            bytes_accessed=6 * units * width + 8 * count * width,
            transcendentals=2 * count * units,
        ),
    )(near, far, pick, gate, up, down)


def with_gates(moe_in, expert_ids, gate_values, experts):
    f32, low = jnp.float32, jnp.bfloat16
    named = jnp.arange(experts, dtype=jnp.int32)[None, None, :] == expert_ids[:, :, None]
    rest = jnp.sum(jnp.where(named, gate_values[:, :, None], 0.0), axis=1)
    columns = [moe_in]
    for _ in range(3):
        top = lax.reduce_precision(rest, 8, 7)
        columns.append(top.astype(low))
        rest = rest - top
    width = moe_in.shape[1] + 3 * experts
    padded = -(-width // LANES) * LANES
    columns.append(jnp.zeros((moe_in.shape[0], padded - width), low))
    return jnp.concatenate(columns, axis=1)


def dense_experts(moe_in, expert_ids, gate_values, gate_weight, up_weight, down_weight):
    low = jnp.bfloat16
    experts = lax.axis_size("context") // CSPLIT
    features = moe_in.shape[1]
    tokens = with_gates(moe_in, expert_ids, gate_values, experts)
    edge = features // LANES * LANES
    columns = jnp.arange(edge, tokens.shape[1], dtype=jnp.int32) - features
    mine = columns % experts == lax.axis_index("context") // CSPLIT
    mine = mine & (columns >= 0) & (columns < 3 * experts)
    pick = mine.astype(jnp.float32)[None, :]
    weights = (gate_weight.T, up_weight.T, down_weight)
    orders = ("zxyc", "yzxc")
    rows = tokens.shape[0] // len(orders)
    sums = []
    for piece, order in enumerate(orders):
        early = gathered(tokens[piece * rows : (piece + 1) * rows], order[:3])
        joined = []
        for block in early:
            near, far = expert_rows(block, from_offset(block, 0, 0, 1), pick, *weights)
            joined.append(added([near, from_offset(far, 0, 0, 1)]).astype(low))
        sums.append(scattered(joined, order[:3]))
    return jnp.concatenate(sums, axis=0)


def rms_scaled(hidden_in, moe_gain):
    scaling = lax.rsqrt(jnp.mean(jnp.square(hidden_in), axis=-1, keepdims=True) + 1e-06)
    return (hidden_in * scaling * moe_gain).astype(jnp.bfloat16)


def on_device(
    residual,
    query_rows,
    key_rows,
    value_rows,
    norm_gain,
    out_weight,
    moe_gain,
    expert_ids,
    gate_values,
    gate_weight,
    up_weight,
    down_weight,
):
    token_count = query_rows.shape[0]
    head_count = query_rows.shape[1] // HD
    query_heads = query_rows.reshape(token_count, head_count, HD)
    key_heads = key_rows.reshape(token_count, head_count, HD)
    value_heads = value_rows.reshape(token_count, head_count, HD)
    own_state = jnp.einsum(
        "shd,she->hde", key_heads, value_heads, preferred_element_type=jnp.float32
    )
    carried = entering(own_state)
    scores = jnp.einsum("thd,shd->hts", query_heads, key_heads, preferred_element_type=jnp.float32)
    causal = jnp.arange(token_count)[:, None] >= jnp.arange(token_count)[None, :]
    weights = jnp.where(causal[None], scores, 0.0).astype(jnp.bfloat16)
    inner_part = jnp.einsum(
        "hts,shd->thd", weights, value_heads, preferred_element_type=jnp.float32
    )
    outer_part = jnp.einsum(
        "thd,hde->the",
        query_heads,
        carried,
        preferred_element_type=jnp.float32,
    )
    mixed = inner_part + outer_part
    center = jnp.mean(mixed, axis=-1, keepdims=True)
    spread = jnp.mean(jnp.square(mixed - center), axis=-1, keepdims=True)
    heads_normed = (
        (mixed - center) * lax.rsqrt(spread + 1e-05) * norm_gain.reshape(head_count, HD)
    ).astype(jnp.bfloat16)
    heads_normed = heads_normed.reshape(token_count, head_count * HD)
    partial_value = jnp.dot(heads_normed, out_weight, preferred_element_type=jnp.float32)
    share = token_count // lax.axis_size("heads")
    offset = lax.axis_index("heads") * share
    if lax.axis_size("context") // CSPLIT <= 2 * expert_ids.shape[1]:
        attended = lax.dynamic_slice_in_dim(residual, offset, share, 0).astype(jnp.float32)
        attended = attended + heads_scattered(partial_value, share)
        moe_part = dense_experts(
            rms_scaled(attended, moe_gain),
            lax.dynamic_slice_in_dim(expert_ids, offset, share, 0),
            lax.dynamic_slice_in_dim(gate_values, offset, share, 0),
            gate_weight[0],
            up_weight[0],
            down_weight[0],
        )
        return (attended + moe_part).astype(jnp.bfloat16)
    attended_all = residual.astype(jnp.float32) + lax.psum(
        partial_value.astype(jnp.bfloat16), "heads"
    ).astype(jnp.float32)
    moe_in = rms_scaled(attended_all, moe_gain)
    attended = lax.dynamic_slice_in_dim(attended_all, offset, share, 0)
    pair_count = CSPLIT
    expert_count = lax.axis_size("context") // CSPLIT
    top_count = expert_ids.shape[1]
    feature_count = moe_in.shape[1]
    capacity = min(token_count, 3 * token_count * top_count // (2 * expert_count))
    flattened = expert_ids.reshape(-1)
    onehot = (flattened[:, None] == jnp.arange(expert_count, dtype=jnp.int32)[None, :]).astype(
        jnp.int32
    )
    ranks = jnp.sum((jnp.cumsum(onehot, axis=0) - onehot) * onehot, axis=1).reshape(
        token_count, top_count
    )
    positions = expert_ids * capacity + ranks
    placer = jnp.any(
        jnp.arange(expert_count * capacity, dtype=jnp.int32)[:, None, None] == positions[None],
        axis=2,
    ).astype(jnp.bfloat16)
    packed = jnp.dot(placer, moe_in, preferred_element_type=jnp.float32).astype(jnp.bfloat16)
    packed = packed.reshape(expert_count, capacity, feature_count)
    half_cap = capacity // pair_count
    outgoing = packed.reshape(expert_count * pair_count, half_cap, feature_count)
    arrived = lax.all_to_all(outgoing, "context", split_axis=0, concat_axis=0, tiled=True)
    partner = partner_2(arrived, "context", 0)
    lower = lax.axis_index("context") % 2 == 0
    first_half = jnp.where(lower, arrived, partner)
    second_half = jnp.where(lower, partner, arrived)
    arrived = jnp.stack([first_half, second_half], axis=2)
    token_rows = arrived.reshape(-1, arrived.shape[-1])
    gate_act = jnp.dot(token_rows, gate_weight[0], preferred_element_type=jnp.float32)
    up_act = jnp.dot(token_rows, up_weight[0], preferred_element_type=jnp.float32)
    hidden = (jax.nn.silu(gate_act) * up_act).astype(jnp.bfloat16)
    partial_rows = jnp.dot(hidden, down_weight[0], preferred_element_type=jnp.float32).astype(
        jnp.bfloat16
    )
    returned = lax.all_to_all(
        partial_rows.reshape(arrived.shape), "context", split_axis=0, concat_axis=0, tiled=True
    )
    slot_offset = ranks % half_cap * pair_count + ranks // half_cap
    flat_return = returned.reshape(-1, feature_count)
    member = jnp.arange(pair_count, dtype=jnp.int32)
    row_index = (
        expert_ids[:, :, None] * pair_count + member[None, None, :]
    ) * capacity + slot_offset[:, :, None]
    picked = jnp.take(flat_return, row_index.reshape(-1), axis=0).reshape(
        token_count, top_count * pair_count, feature_count
    )
    mix_weights = jnp.repeat(gate_values, pair_count, axis=1)
    mixture = jnp.sum(mix_weights[:, :, None] * picked.astype(jnp.float32), axis=1)
    moe_part = lax.psum_scatter(
        mixture.astype(jnp.bfloat16), "heads", scatter_dimension=0, tiled=True
    ).astype(jnp.float32)
    return (attended + moe_part).astype(jnp.bfloat16)


def solution(mesh):
    in_specs = (
        P("context", None),
        P("context", "heads"),
        P("context", "heads"),
        P("context", "heads"),
        P("heads"),
        P("heads", None),
        P(),
        P("context", None),
        P("context", None),
        P("context", None, "heads"),
        P("context", None, "heads"),
        P("context", "heads", None),
    )
    out_specs = P(("context", "heads"), None)
    return jax.shard_map(
        on_device, mesh=mesh, in_specs=in_specs, out_specs=out_specs, check_vma=False
    )
```

```python
import jax
import jax.numpy as jnp
from jax import lax
from jax.experimental import pallas as pl
from jax.experimental.pallas import tpu as pltpu
from jax.sharding import PartitionSpec as P

HD = 64
CSPLIT = 2
LANES = 128


def partner_2(value, axis, apart):
    mask = 2**apart
    pairs = [(source, source ^ mask) for source in range(lax.axis_size(axis))]
    return lax.ppermute(value, axis, pairs)


def grid_of():
    across = lax.axis_size("heads")
    along = lax.axis_size("context") // (CSPLIT * across)
    index = lax.axis_index("context")
    return along, across, index // (CSPLIT * across), index // CSPLIT % across, index % CSPLIT


def from_offset(value, dz, dx, dc, wrap=True):
    along, across = grid_of()[:2]
    pairs = []
    for z in range(along):
        for x in range(across):
            for core in range(CSPLIT):
                if not wrap and not 0 <= z + dz < along:
                    continue
                source = (((z + dz) % along) * across + (x + dx) % across) * CSPLIT
                source += (core + dc) % CSPLIT
                pairs.append((source, (z * across + x) * CSPLIT + core))
    return lax.ppermute(value, "context", pairs)


def from_heads(value, d):
    count = lax.axis_size("heads")
    return lax.ppermute(value, "heads", [((h + d) % count, h) for h in range(count)])


def entering(own):
    along, across, _, x, core = grid_of()
    f32, low = jnp.float32, jnp.bfloat16
    heads = own.shape[0] // 2
    packed = jnp.concatenate([own[:heads], own[heads:]], axis=-1).astype(low)
    other = from_offset(packed, 0, 0, 1)
    before = jnp.where(core == 1, other, jnp.zeros_like(other)).astype(f32)
    pair = packed.astype(f32) + other.astype(f32)
    rows = packed.shape[1] // CSPLIT
    total = lax.dynamic_slice_in_dim(pair, core * rows, rows, 1)
    half = total.astype(low)
    earlier = jnp.zeros_like(total)
    for d in range(1, across):
        part = from_offset(half, 0, d, 0).astype(f32)
        total = total + part
        earlier = earlier + jnp.where(x + d >= across, part, 0.0)
    plane = total.astype(low)
    for d in range(1, along):
        earlier = earlier + from_offset(plane, -d, 0, 0, wrap=False).astype(f32)
    mine = earlier.astype(low)
    theirs = from_offset(mine, 0, 0, 1)
    lower = jnp.where(core == 0, mine, theirs)
    upper = jnp.where(core == 0, theirs, mine)
    before = (before + jnp.concatenate([lower, upper], axis=1).astype(f32)).astype(low)
    return jnp.concatenate([before[:, :, :HD], before[:, :, HD:]], axis=0)


def heads_scattered(partial, share):
    count, me = lax.axis_size("heads"), lax.axis_index("heads")
    total = lax.dynamic_slice_in_dim(partial, me * share, share, 0)
    low = partial.astype(jnp.bfloat16)
    for d in range(1, count):
        start = (me + count - d) % count * share
        sent = lax.dynamic_slice_in_dim(low, start, share, 0)
        total = total + from_heads(sent, d).astype(jnp.float32)
    return total


def steps_of(kind):
    along, across = grid_of()[:2]
    count = {"z": along, "x": across, "y": lax.axis_size("heads"), "c": CSPLIT}[kind]

    def step(value, d):
        if kind == "y":
            return from_heads(value, d)
        return from_offset(value, *[d if kind == name else 0 for name in "zxc"])

    return count, step


def spread(rows, kind):
    count, step = steps_of(kind)
    return [rows] + [step(rows, d) for d in range(1, count)]


def after(value, other):
    return lax.optimization_barrier((value, other))[0]


def added(parts):
    total = parts[0].astype(jnp.float32)
    for part in parts[1:]:
        total = total + part.astype(jnp.float32)
    return total


def scattered(parts, order):
    for kind in reversed(order):
        count, step = steps_of(kind)
        if not isinstance(parts, list):
            rows = parts.shape[0] // count
            parts = [parts[d * rows : (d + 1) * rows] for d in range(count)]
        moved = [step(parts[d], count - d) for d in range(1, count)]
        total = added([parts[0]] + moved)
        parts = total.astype(jnp.bfloat16) if kind != order[0] else total
    return parts


def expert_kernel(near, far, pick, gate, up, down, near_out, far_out, total):
    step, last = pl.program_id(0), pl.num_programs(0) - 1
    width = gate.shape[1]
    edge = width // LANES * LANES
    f32 = jnp.float32
    across = (((1,), (1,)), ((), ()))
    for turn, (rows, out) in enumerate(((near, near_out), (far, far_out))):
        tokens = rows[:, :width]
        gate_act = lax.dot_general(tokens, gate[...], across, preferred_element_type=f32)
        up_act = lax.dot_general(tokens, up[...], across, preferred_element_type=f32)
        hidden = (gate_act / (1.0 + jnp.exp(-gate_act)) * up_act).astype(jnp.bfloat16)
        part = jnp.dot(hidden, down[...], preferred_element_type=f32)

        @pl.when(step == 0)
        def _():
            total[turn] = part

        @pl.when(step > 0)
        def _():
            total[turn] += part

        @pl.when(step == last)
        def _():
            weight = rows[:, edge:].astype(f32) * pick[...]
            weight = jnp.sum(weight, axis=1, keepdims=True)
            out[:, edge:] = jnp.zeros((out.shape[0], out.shape[1] - edge), out.dtype)
            out[:, :width] = (total[turn] * weight).astype(out.dtype)


def expert_rows(near, far, pick, gate, up, down):
    units, width = down.shape
    tile = max(t for t in range(16, 257, 16) if units % t == 0)
    fixed = lambda shape: pl.BlockSpec(shape, lambda i: (0, 0), pipeline_mode=pl.Buffered(1))
    tiles = pl.BlockSpec((tile, width), lambda i: (i, 0))
    count = near.shape[0]
    result = jax.ShapeDtypeStruct(near.shape, near.dtype)
    return pl.pallas_call(
        expert_kernel,
        grid=(units // tile,),
        in_specs=[fixed(near.shape), fixed(far.shape), fixed(pick.shape), tiles, tiles, tiles],
        out_specs=[fixed(result.shape)] * 2,
        out_shape=[result] * 2,
        scratch_shapes=[pltpu.VMEM((2, count, width), jnp.float32)],
        compiler_params=pltpu.CompilerParams(vmem_limit_bytes=48 * 2**20),
        cost_estimate=pl.CostEstimate(
            flops=12 * count * units * width,
            bytes_accessed=6 * units * width + 8 * count * width,
            transcendentals=2 * count * units,
        ),
    )(near, far, pick, gate, up, down)


def with_gates(moe_in, expert_ids, gate_values, experts):
    low = jnp.bfloat16
    named = jnp.arange(experts, dtype=jnp.int32)[None, None, :] == expert_ids[:, :, None]
    rest = jnp.sum(jnp.where(named, gate_values[:, :, None], 0.0), axis=1)
    columns = [moe_in]
    for _ in range(3):
        top = lax.reduce_precision(rest, 8, 7)
        columns.append(top.astype(low))
        rest = rest - top
    width = moe_in.shape[1] + 3 * experts
    padded = -(-width // LANES) * LANES
    columns.append(jnp.zeros((moe_in.shape[0], padded - width), low))
    return jnp.concatenate(columns, axis=1)


def dense_experts(moe_in, expert_ids, gate_values, gate_weight, up_weight, down_weight):
    low = jnp.bfloat16
    experts = lax.axis_size("context") // CSPLIT
    features = moe_in.shape[1]
    tokens = with_gates(moe_in, expert_ids, gate_values, experts)
    edge = features // LANES * LANES
    columns = jnp.arange(edge, tokens.shape[1], dtype=jnp.int32) - features
    mine = columns % experts == lax.axis_index("context") // CSPLIT
    mine = mine & (columns >= 0) & (columns < 3 * experts)
    pick = mine.astype(jnp.float32)[None, :]
    weights = (gate_weight.T, up_weight.T, down_weight)
    rows = tokens.shape[0] // 2

    def run(block):
        other = from_offset(block, 0, 0, 1)
        near, far = expert_rows(block, other, pick, *weights)
        return near, from_offset(far, 0, 0, 1)

    def joined(pairs):
        return [added(pair).astype(low) for pair in pairs]

    def stacked(parts):
        return jnp.concatenate(parts, axis=0)

    first = stacked(spread(tokens[:rows], "z"))
    second = after(stacked(spread(tokens[rows:], "y")), first)
    first = spread(stacked(spread(first, "x")), "y")
    second = stacked(spread(second, "z"))
    first_out, second_out = [run(first[0])], []
    second = spread(after(second, first_out[0][0]), "x")
    second_out.append(run(second[0]))
    for block in first[1:]:
        first_out.append(run(after(block, second_out[0][0])))
    for block in second[1:]:
        second_out.append(run(after(block, first_out[-1][0])))
    first_sum = scattered(joined(first_out), "zxy")
    second_sum = scattered(joined(second_out), "yzx")
    return stacked([first_sum, second_sum])[:, :features]


def rms_scaled(hidden_in, moe_gain):
    scaling = lax.rsqrt(jnp.mean(jnp.square(hidden_in), axis=-1, keepdims=True) + 1e-06)
    return (hidden_in * scaling * moe_gain).astype(jnp.bfloat16)


def on_device(
    residual,
    query_rows,
    key_rows,
    value_rows,
    norm_gain,
    out_weight,
    moe_gain,
    expert_ids,
    gate_values,
    gate_weight,
    up_weight,
    down_weight,
):
    token_count = query_rows.shape[0]
    head_count = query_rows.shape[1] // HD
    query_heads = query_rows.reshape(token_count, head_count, HD)
    key_heads = key_rows.reshape(token_count, head_count, HD)
    value_heads = value_rows.reshape(token_count, head_count, HD)
    own_state = jnp.einsum(
        "shd,she->hde", key_heads, value_heads, preferred_element_type=jnp.float32
    )
    carried = entering(own_state)
    scores = jnp.einsum("thd,shd->hts", query_heads, key_heads, preferred_element_type=jnp.float32)
    causal = jnp.arange(token_count)[:, None] >= jnp.arange(token_count)[None, :]
    weights = jnp.where(causal[None], scores, 0.0).astype(jnp.bfloat16)
    inner_part = jnp.einsum(
        "hts,shd->thd", weights, value_heads, preferred_element_type=jnp.float32
    )
    outer_part = jnp.einsum(
        "thd,hde->the",
        query_heads,
        carried,
        preferred_element_type=jnp.float32,
    )
    mixed = inner_part + outer_part
    center = jnp.mean(mixed, axis=-1, keepdims=True)
    spread = jnp.mean(jnp.square(mixed - center), axis=-1, keepdims=True)
    heads_normed = (
        (mixed - center) * lax.rsqrt(spread + 1e-05) * norm_gain.reshape(head_count, HD)
    ).astype(jnp.bfloat16)
    heads_normed = heads_normed.reshape(token_count, head_count * HD)
    partial_value = jnp.dot(heads_normed, out_weight, preferred_element_type=jnp.float32)
    share = token_count // lax.axis_size("heads")
    offset = lax.axis_index("heads") * share
    if lax.axis_size("context") // CSPLIT <= 2 * expert_ids.shape[1]:
        attended = lax.dynamic_slice_in_dim(residual, offset, share, 0).astype(jnp.float32)
        attended = attended + heads_scattered(partial_value, share)
        moe_part = dense_experts(
            rms_scaled(attended, moe_gain),
            lax.dynamic_slice_in_dim(expert_ids, offset, share, 0),
            lax.dynamic_slice_in_dim(gate_values, offset, share, 0),
            gate_weight[0],
            up_weight[0],
            down_weight[0],
        )
        return (attended + moe_part).astype(jnp.bfloat16)
    attended_all = residual.astype(jnp.float32) + lax.psum(
        partial_value.astype(jnp.bfloat16), "heads"
    ).astype(jnp.float32)
    moe_in = rms_scaled(attended_all, moe_gain)
    attended = lax.dynamic_slice_in_dim(attended_all, offset, share, 0)
    pair_count = CSPLIT
    expert_count = lax.axis_size("context") // CSPLIT
    top_count = expert_ids.shape[1]
    feature_count = moe_in.shape[1]
    capacity = min(token_count, 3 * token_count * top_count // (2 * expert_count))
    flattened = expert_ids.reshape(-1)
    onehot = (flattened[:, None] == jnp.arange(expert_count, dtype=jnp.int32)[None, :]).astype(
        jnp.int32
    )
    ranks = jnp.sum((jnp.cumsum(onehot, axis=0) - onehot) * onehot, axis=1).reshape(
        token_count, top_count
    )
    positions = expert_ids * capacity + ranks
    placer = jnp.any(
        jnp.arange(expert_count * capacity, dtype=jnp.int32)[:, None, None] == positions[None],
        axis=2,
    ).astype(jnp.bfloat16)
    packed = jnp.dot(placer, moe_in, preferred_element_type=jnp.float32).astype(jnp.bfloat16)
    packed = packed.reshape(expert_count, capacity, feature_count)
    half_cap = capacity // pair_count
    outgoing = packed.reshape(expert_count * pair_count, half_cap, feature_count)
    arrived = lax.all_to_all(outgoing, "context", split_axis=0, concat_axis=0, tiled=True)
    partner = partner_2(arrived, "context", 0)
    lower = lax.axis_index("context") % 2 == 0
    first_half = jnp.where(lower, arrived, partner)
    second_half = jnp.where(lower, partner, arrived)
    arrived = jnp.stack([first_half, second_half], axis=2)
    token_rows = arrived.reshape(-1, arrived.shape[-1])
    gate_act = jnp.dot(token_rows, gate_weight[0], preferred_element_type=jnp.float32)
    up_act = jnp.dot(token_rows, up_weight[0], preferred_element_type=jnp.float32)
    hidden = (jax.nn.silu(gate_act) * up_act).astype(jnp.bfloat16)
    partial_rows = jnp.dot(hidden, down_weight[0], preferred_element_type=jnp.float32).astype(
        jnp.bfloat16
    )
    returned = lax.all_to_all(
        partial_rows.reshape(arrived.shape), "context", split_axis=0, concat_axis=0, tiled=True
    )
    slot_offset = ranks % half_cap * pair_count + ranks // half_cap
    flat_return = returned.reshape(-1, feature_count)
    member = jnp.arange(pair_count, dtype=jnp.int32)
    row_index = (
        expert_ids[:, :, None] * pair_count + member[None, None, :]
    ) * capacity + slot_offset[:, :, None]
    picked = jnp.take(flat_return, row_index.reshape(-1), axis=0).reshape(
        token_count, top_count * pair_count, feature_count
    )
    mix_weights = jnp.repeat(gate_values, pair_count, axis=1)
    mixture = jnp.sum(mix_weights[:, :, None] * picked.astype(jnp.float32), axis=1)
    moe_part = lax.psum_scatter(
        mixture.astype(jnp.bfloat16), "heads", scatter_dimension=0, tiled=True
    ).astype(jnp.float32)
    return (attended + moe_part).astype(jnp.bfloat16)


def solution(mesh):
    in_specs = (
        P("context", None),
        P("context", "heads"),
        P("context", "heads"),
        P("context", "heads"),
        P("heads"),
        P("heads", None),
        P(),
        P("context", None),
        P("context", None),
        P("context", None, "heads"),
        P("context", None, "heads"),
        P("context", "heads", None),
    )
    out_specs = P(("context", "heads"), None)
    return jax.shard_map(
        on_device, mesh=mesh, in_specs=in_specs, out_specs=out_specs, check_vma=False
    )
```
